32 devices in a mesh: req: 16 (over z, y, x), tp: 2 (over core).
Axes of the slice: x: 2, y: 2, z: 4, core: 2. Of those that a mesh axis runs over, the one named last changes fastest.
Arguments:
- hidden: bfloat16 [16, 32, 2048], P('req', 'tp'), may hold values from -4.5 to 4.5
- norm_gain: float32 [2048], replicated, may hold values from 0.1 to 1.9
- embedding: bfloat16 [16384, 2048], P(('req', 'tp')), may hold values from -0.79549513 to 0.79549513
- target_ids: int32 [16, 32], P('req', 'tp'), may hold values from 0 to 16383
- lengths: int32 [16], P('req'), may hold values from 1 to 32, 320 in all
- response_mask: int32 [16, 32], P('req', 'tp'), may hold values 0 or 1
Outputs:
- logprob: float32 [16, 32], P('req', 'tp')
- entropy: float32 [16, 32], P('req', 'tp')
The draws below stay inside these ranges and needn't reach their ends.
All inputs are finite; a program needn't handle non-finite values. No bound on the sum of `lengths` or of `response_mask` on one device may be relied on, other than what follows from the above.
Results may differ from the reference program's by a relative error of at most 0.0027.
Values may be sent and summed in bfloat16 or wider, within the bound.
A program may use at most 64 MiB of HBM per device.

```python
import math
import jax
import jax.numpy as jnp
import numpy as np
from jax import lax

D = 2048
VOC_DEV = 512
CAP = 32
SEQS = 16
TOKENS = 512
VOCAB = 16384
N_REQ = 16
N_TP = 2


def unit_row(key, vocab_id):
    inner = jax.random.fold_in(jax.random.fold_in(key, 71), vocab_id)
    return jax.random.truncated_normal(inner, -4.0, 4.0, (D,), jnp.float32)


def draw_target_ids(key, part):
    return jax.random.randint(jax.random.fold_in(key, 29), (SEQS, CAP), 0, VOCAB, dtype=jnp.int32)


def draw_embedding(key, part):
    units = jax.vmap(lambda v: unit_row(key, v))(jnp.arange(VOCAB, dtype=jnp.int32))
    spread = 0.8
    logs = jax.random.uniform(jax.random.fold_in(key, 73), (VOCAB, 1), jnp.float32, -spread, spread)
    return (units * jnp.exp(logs) * (3.0 / math.sqrt(D))).astype(jnp.bfloat16)


def draw_hidden(key, part):
    targets = draw_target_ids(key, part).reshape(-1)
    units = jax.vmap(lambda v: unit_row(key, v))(targets).reshape(SEQS, CAP, D)
    weight = 4.0 / math.sqrt(D)
    noise = jax.random.truncated_normal(jax.random.fold_in(key, 83), -4.0, 4.0, (SEQS, CAP, D), jnp.float32)
    return (weight * units + noise).astype(jnp.bfloat16)


def plant(drawn, key, smallest, top_value):
    shape = drawn.shape
    spot = [jax.random.randint(jax.random.fold_in(key, axis), (), 0, shape[axis]) for axis in range(len(shape))]
    drawn = drawn.at[tuple(spot)].set(smallest)
    longest = shape.index(max(shape))
    spot[longest] = (spot[longest] + 1) % shape[longest]
    return drawn.at[tuple(spot)].set(top_value)


def length_profile(amount, total, bound, lean):
    loads = [(1 << 20) // math.isqrt(standing ** lean) + 1 for standing in range(2, amount + 1)]
    surplus, given = total - bound - (amount - 1), [1] * (amount - 1)
    while surplus > 0:
        candidates = [i for i in range(amount - 1) if given[i] < bound]
        whole, budget = sum([loads[i] for i in candidates]), surplus
        for i in candidates:
            extra = min(bound - given[i], max(1, budget * loads[i] // whole), surplus)
            given[i] = given[i] + extra
            surplus = surplus - extra
    return np.array([bound] + given)


def ragged(key, amount, total, limit, lean):
    if amount == 2:
        one = jax.random.randint(key, (), max(1, total - limit), min(limit, total - 1) + 1)
        return jnp.stack([one, total - one])
    sizes = jnp.asarray(length_profile(amount, total, limit, lean), jnp.int32)
    pairs = (amount - 1) // 2
    giver, receiver = sizes[1:1 + 2 * pairs:2], sizes[2:2 + 2 * pairs:2]
    slack = jnp.minimum(giver - 1, limit - receiver)
    moved = jax.random.randint(jax.random.fold_in(key, 1), (pairs,), 0, 1 << 20) % (slack + 1)
    sizes = sizes.at[1:1 + 2 * pairs:2].set(giver - moved).at[2:2 + 2 * pairs:2].set(receiver + moved)
    return sizes[jax.random.permutation(jax.random.fold_in(key, 2), amount)]


def setup_inputs(seed: int = 0) -> dict:
    key_list = jax.random.split(jax.random.key(seed), 7)
    hidden = draw_hidden(jax.random.fold_in(key_list[6], 71), 0)
    norm_gain = jnp.clip(1.0 + 0.18 * jax.random.normal(key_list[1], (D,), jnp.float32), 0.1, 1.9)
    embedding = draw_embedding(jax.random.fold_in(key_list[6], 71), 0)
    target_ids = draw_target_ids(jax.random.fold_in(key_list[6], 71), 0)
    lengths = ragged(key_list[4], SEQS, N_REQ * CAP * 5 // 8, CAP, 1).astype(jnp.int32)
    response_mask = plant((jax.random.randint(key_list[5], (SEQS, CAP), 0, 4) < 3).astype(jnp.int32), jax.random.fold_in(key_list[5], 1), 0, 1)
    return {"hidden": hidden, "norm_gain": norm_gain, "embedding": embedding, "target_ids": target_ids, "lengths": lengths, "response_mask": response_mask}


def reference(hidden, norm_gain, embedding, target_ids, lengths, response_mask):
    rows = hidden.astype(jnp.float32).reshape(TOKENS, D)
    scale = lax.rsqrt(lax.optimization_barrier(jnp.mean(rows * rows, axis=1, keepdims=True)) + 1e-06)
    normed = (rows * scale * norm_gain[None, :]).astype(jnp.bfloat16)
    targets = target_ids.reshape(TOKENS)
    block_rows = VOC_DEV * N_TP
    blocks = embedding.reshape(VOCAB // block_rows, block_rows, D)
    starts = (jnp.arange(VOCAB // block_rows) * block_rows).astype(jnp.int32)

    def visit(carry, inputs):
        table, start = inputs
        raw = lax.dot_general(normed, table, (((1,), (1,)), ((), ())), preferred_element_type=jnp.float32)
        logits = 30.0 * jnp.tanh(raw / 30.0)
        expo = jnp.exp(logits)
        ident = start + lax.broadcasted_iota(jnp.int32, (1, block_rows), 1)
        hit = jnp.where(ident == targets[:, None], logits, jnp.float32(0.0))
        return ((carry[0] + lax.optimization_barrier(jnp.sum(expo, axis=1)), carry[1] + lax.optimization_barrier(jnp.sum(expo * logits, axis=1)), carry[2] + lax.optimization_barrier(jnp.sum(hit, axis=1))), None)
    zeros = jnp.zeros((TOKENS,), jnp.float32)
    (total, moment, picked), unused = lax.scan(visit, (zeros, zeros, zeros), (blocks, starts))
    lse = jnp.log(total)
    position = lax.broadcasted_iota(jnp.int32, (SEQS, CAP), 1)
    scored = (response_mask == 1) & (position < lengths[:, None])
    logprob = jnp.where(scored, (picked - lse).reshape(SEQS, CAP), jnp.float32(0.0))
    entropy = jnp.where(scored, (lse - moment / total).reshape(SEQS, CAP), jnp.float32(0.0))
    return (logprob, entropy)
```

```python
import functools

import jax
import jax.numpy as jnp
from jax import lax
from jax.experimental import pallas as pl
from jax.experimental.pallas import tpu as pltpu
from jax.sharding import PartitionSpec as P

MESH = pl.DeviceIdType.MESH
SPECS = dict(
    in_specs=(
        P("req", "tp", None),
        P(),
        P(("req", "tp"), None),
        P("req", "tp"),
        P("req"),
        P("req", "tp"),
    ),
    out_specs=(P("req", "tp"), P("req", "tp")),
    check_vma=False,
)


def vocab_sums(states, targets, table, vocab_start):
    raw = lax.dot_general(
        states, table, (((1,), (1,)), ((), ())), preferred_element_type=jnp.float32
    )
    logits = 30.0 * jnp.tanh(raw / 30.0)
    expo = jnp.exp(logits)
    ident = vocab_start + lax.broadcasted_iota(jnp.int32, (1, table.shape[0]), 1)
    hit = jnp.where(ident == targets[:, None], logits, jnp.float32(0.0))
    return (jnp.sum(expo, axis=1), jnp.sum(expo * logits, axis=1), jnp.sum(hit, axis=1))


def on_device(hidden, norm_gain, embedding, target_ids, lengths, response_mask):
    seq_here, slots, width = hidden.shape
    rows = hidden.reshape(seq_here * slots, width).astype(jnp.float32)
    scale = lax.rsqrt(jnp.mean(rows * rows, axis=1, keepdims=True) + 1e-06)
    normed = (rows * scale * norm_gain[None, :]).astype(jnp.bfloat16)
    targets = target_ids.reshape(seq_here * slots)
    vocab_start = lax.axis_index(("req", "tp")) * embedding.shape[0]
    sums = vocab_sums(
        lax.all_gather(normed, ("req", "tp"), axis=0, tiled=True),
        lax.all_gather(targets, ("req", "tp"), axis=0, tiled=True),
        embedding,
        vocab_start,
    )
    total, moment, picked = (
        lax.psum_scatter(s, ("req", "tp"), scatter_dimension=0, tiled=True) for s in sums
    )
    lse = jnp.log(total)
    position = lax.axis_index("tp") * slots + lax.broadcasted_iota(jnp.int32, (seq_here, slots), 1)
    scored = (response_mask == 1) & (position < lengths[:, None])
    logprob = jnp.where(scored, (picked - lse).reshape(seq_here, slots), jnp.float32(0.0))
    entropy = jnp.where(scored, (lse - moment / total).reshape(seq_here, slots), jnp.float32(0.0))
    return (logprob, entropy)


def J(b, a, area, dz):
    return b * 16 + a * 8 + area * 4 + dz


def kernel(slots, hidden_ref, gain_ref, target_ref, length_ref, mask_ref, emb_hbm,
           lp_ref, ent_ref, emb, X, part, R, emb_sem, xs, xr, rs, rr):
    width = hidden_ref.shape[1]
    voc = emb.shape[0]
    q, c = lax.axis_index("req"), lax.axis_index("tp")
    x, y, z = q % 2, (q // 2) % 2, q // 4

    def device(dz, fa, fb, core):
        fx, fy = fa * (1 - c) + fb * c, fb * (1 - c) + fa * c
        nx, ny = x + fx * (1 - 2 * x), y + fy * (1 - 2 * y)
        nz = (z, z + 1 - 2 * (z % 2), z + 2 - 4 * (z // 2), 3 - z)[dz]
        return (nz * 4 + ny * 2 + nx, core)

    load = pltpu.make_async_copy(emb_hbm, emb, emb_sem)
    load.start()
    barrier = pltpu.get_barrier_semaphore()
    near = [device(1, 0, 0, c), device(2, 0, 0, c), device(3, 0, 0, c),
            device(0, 1, 0, c), device(0, 0, 1, c), device(0, 0, 0, 1 - c)]
    for d in near:
        pl.semaphore_signal(barrier, inc=1, device_id=d, device_id_type=MESH)

    rows = hidden_ref[...].astype(jnp.float32)
    scale = lax.rsqrt(jnp.mean(rows * rows, axis=1, keepdims=True) + 1e-06)
    X[0:slots, 0:width] = (rows * scale * gain_ref[...]).astype(jnp.bfloat16)
    tgt = jnp.broadcast_to(target_ref[...], (slots, slots))
    eye = lax.broadcasted_iota(jnp.int32, (slots, slots), 0) == lax.broadcasted_iota(
        jnp.int32, (slots, slots), 1)
    tcol = jnp.sum(jnp.where(eye, tgt, 0).astype(jnp.float32), axis=1, keepdims=True)
    high = jnp.floor(tcol * (1.0 / 256.0))
    low = tcol - high * 256.0
    lane = lax.broadcasted_iota(jnp.int32, (slots, 128), 1)
    X[0:slots, width:width + 128] = jnp.where(
        lane == 0, high, jnp.where(lane == 1, low, 0.0)).astype(jnp.bfloat16)
    pl.semaphore_wait(barrier, len(near))

    def block(slot):
        return X.at[pl.ds(slot * slots, slots), :]

    sends = []

    def send(src, dst, dev):
        copy = pltpu.make_async_remote_copy(
            src_ref=block(src), dst_ref=block(dst), send_sem=xs.at[len(sends)],
            recv_sem=xr.at[dst], device_id=dev, device_id_type=MESH)
        copy.start()
        sends.append(copy)

    def arrived(slot):
        pltpu.make_async_remote_copy(
            src_ref=block(slot), dst_ref=block(slot), send_sem=xs.at[0],
            recv_sem=xr.at[slot], device_id=near[5], device_id_type=MESH).wait_recv()

    def forward(b, a, dz):
        if b == 0 and a == 0:
            send(J(0, 0, 0, dz), J(0, 1, 0, dz), near[3])
        if b == 0:
            send(J(0, a, 0, dz), J(1, a, 0, dz), near[4])
        send(J(b, a, 0, dz), J(b, a, 1, dz), near[5])

    def relay(b, a, dz):
        arrived(J(b, a, 0, dz))
        forward(b, a, dz)

    start = ((q * 2 + c) * voc).astype(jnp.float32)
    outs = []

    def group(b, a):
        for dz in range(4):
            arrived(J(b, a, 1, dz))
        base = J(b, a, 0, 0) * slots
        g = b * 2 + a
        toks = 8 * slots
        pick = lax.broadcasted_iota(jnp.int32, (8, 128), 1)
        pick = jnp.where(pick == 0, 256.0, jnp.where(pick == 1, 1.0, 0.0)).astype(jnp.bfloat16)
        target = lax.dot_general(
            pick, X[base:base + toks, width:width + 128], (((1,), (1,)), ((), ())),
            preferred_element_type=jnp.float32)[0:1, :] - start
        raw = lax.dot_general(
            emb[...], X[base:base + toks, 0:width], (((1,), (1,)), ((), ())),
            preferred_element_type=jnp.float32)
        logits = 30.0 * jnp.tanh(raw / 30.0)
        expo = jnp.exp(logits)
        ident = lax.broadcasted_iota(jnp.int32, (voc, toks), 0).astype(jnp.float32)
        part[g, 0:1, :] = jnp.sum(expo, axis=0, keepdims=True)
        part[g, 1:2, :] = jnp.sum(expo * logits, axis=0, keepdims=True)
        part[g, 2:3, :] = jnp.sum(jnp.where(ident == target, logits, 0.0), axis=0, keepdims=True)
        part[g, 3:4, :] = jnp.zeros((1, toks), jnp.float32)
        for area in (1, 0):
            for dz in (3, 2, 1, 0):
                slot = J(b, a, area, dz)
                if slot == 0:
                    continue
                fa, fb = (a, b) if area == 0 else (b, a)
                copy = pltpu.make_async_remote_copy(
                    src_ref=part.at[g], dst_ref=R.at[slot], send_sem=rs.at[slot],
                    recv_sem=rr.at[slot],
                    device_id=device(dz, fa, fb, c if area == 0 else 1 - c),
                    device_id_type=MESH)
                copy.start()
                outs.append(copy)

    for dz in (3, 2, 1):
        send(0, J(0, 0, 0, dz), near[dz - 1])
    forward(0, 0, 0)
    relay(0, 0, 1)
    relay(0, 1, 0)
    relay(0, 0, 2)
    relay(0, 0, 3)
    relay(1, 0, 0)
    relay(0, 1, 1)
    relay(0, 1, 2)
    relay(0, 1, 3)
    load.wait()
    group(0, 0)
    for dz in (1, 2, 3):
        relay(1, 0, dz)
    group(0, 1)
    for dz in range(4):
        relay(1, 1, dz)
    group(1, 0)
    group(1, 1)

    for copy in outs:
        copy.wait_recv()
    home = lax.broadcasted_iota(jnp.int32, (4, 8 * slots), 1) // slots
    acc = None
    for k in range(8):
        s = part[0] if k == 0 else R[k]
        for g in range(1, 4):
            s = s + R[g * 8 + k]
        s = jnp.where(home == k, s, 0.0)
        acc = s if acc is None else acc + s
    for shift in (64, 32, 16):
        acc = acc + pltpu.roll(acc, shift, 1)
    total, moment, picked = (acc[i:i + 1, 0:slots] for i in range(3))
    lse = jnp.log(total)
    position = c * slots + lax.broadcasted_iota(jnp.int32, (1, slots), 1)
    scored = (mask_ref[...] == 1) & (position < length_ref[0])
    lp_ref[...] = jnp.where(scored, picked - lse, 0.0)
    ent_ref[...] = jnp.where(scored, lse - moment / total, 0.0)
    for copy in sends:
        copy.wait_send()
    for copy in outs:
        copy.wait_send()


def fused(hidden, norm_gain, embedding, target_ids, lengths, response_mask):
    _, slots, width = hidden.shape
    voc = embedding.shape[0]
    vmem = pl.BlockSpec(memory_space=pltpu.VMEM)
    out = jax.ShapeDtypeStruct((1, slots), jnp.float32)
    return pl.pallas_call(
        functools.partial(kernel, slots),
        out_shape=(out, out),
        in_specs=[vmem, vmem, vmem, pl.BlockSpec(memory_space=pltpu.SMEM), vmem,
                  pl.BlockSpec(memory_space=pl.ANY)],
        out_specs=(vmem, vmem),
        scratch_shapes=[
            pltpu.VMEM((voc, width), jnp.bfloat16),
            pltpu.VMEM((32 * slots, width + 128), jnp.bfloat16),
            pltpu.VMEM((4, 4, 8 * slots), jnp.float32),
            pltpu.VMEM((32, 4, 8 * slots), jnp.float32),
            pltpu.SemaphoreType.DMA,
            pltpu.SemaphoreType.DMA((32,)),
            pltpu.SemaphoreType.DMA((32,)),
            pltpu.SemaphoreType.DMA((32,)),
            pltpu.SemaphoreType.DMA((32,)),
        ],
        compiler_params=pltpu.CompilerParams(collective_id=0, has_side_effects=True),
    )(hidden.reshape(slots, width), norm_gain.reshape(1, width), target_ids, lengths,
      response_mask, embedding)


def solution(mesh):
    body = fused if dict(mesh.shape) == {"req": 16, "tp": 2} else on_device
    return jax.shard_map(body, mesh=mesh, **SPECS)
```

```python
import functools

import jax
import jax.numpy as jnp
from jax import lax
from jax.experimental import pallas as pl
from jax.experimental.pallas import tpu as pltpu
from jax.sharding import PartitionSpec as P

MESH = pl.DeviceIdType.MESH
SPECS = dict(
    in_specs=(
        P("req", "tp", None),
        P(),
        P(("req", "tp"), None),
        P("req", "tp"),
        P("req"),
        P("req", "tp"),
    ),
    out_specs=(P("req", "tp"), P("req", "tp")),
    check_vma=False,
)


def vocab_sums(states, targets, table, vocab_start):
    raw = lax.dot_general(
        states, table, (((1,), (1,)), ((), ())), preferred_element_type=jnp.float32
    )
    logits = 30.0 * jnp.tanh(raw / 30.0)
    expo = jnp.exp(logits)
    ident = vocab_start + lax.broadcasted_iota(jnp.int32, (1, table.shape[0]), 1)
    hit = jnp.where(ident == targets[:, None], logits, jnp.float32(0.0))
    return (jnp.sum(expo, axis=1), jnp.sum(expo * logits, axis=1), jnp.sum(hit, axis=1))


def on_device(hidden, norm_gain, embedding, target_ids, lengths, response_mask):
    seq_here, slots, width = hidden.shape
    rows = hidden.reshape(seq_here * slots, width).astype(jnp.float32)
    scale = lax.rsqrt(jnp.mean(rows * rows, axis=1, keepdims=True) + 1e-06)
    normed = (rows * scale * norm_gain[None, :]).astype(jnp.bfloat16)
    targets = target_ids.reshape(seq_here * slots)
    vocab_start = lax.axis_index(("req", "tp")) * embedding.shape[0]
    sums = vocab_sums(
        lax.all_gather(normed, ("req", "tp"), axis=0, tiled=True),
        lax.all_gather(targets, ("req", "tp"), axis=0, tiled=True),
        embedding,
        vocab_start,
    )
    total, moment, picked = (
        lax.psum_scatter(s, ("req", "tp"), scatter_dimension=0, tiled=True) for s in sums
    )
    lse = jnp.log(total)
    position = lax.axis_index("tp") * slots + lax.broadcasted_iota(jnp.int32, (seq_here, slots), 1)
    scored = (response_mask == 1) & (position < lengths[:, None])
    logprob = jnp.where(scored, (picked - lse).reshape(seq_here, slots), jnp.float32(0.0))
    entropy = jnp.where(scored, (lse - moment / total).reshape(seq_here, slots), jnp.float32(0.0))
    return (logprob, entropy)


PARTS = 1
RELAYED = ()


def J(b, a, area, s):
    return s * 8 + b * 4 + a * 2 + area


def kernel(slots, hidden_hbm, gain_hbm, target_hbm, mask_hbm, length_hbm, emb_hbm, out_ref,
           hidden, gain, target_row, mask, length, emb, X, part, R,
           load_sem, z_sem, a_sem, b_sem, c_sem, p_sem, xr, rs, rr):
    width = hidden.shape[1]
    voc = emb.shape[0]
    q, c = lax.axis_index("req"), lax.axis_index("tp")
    x, y, z = q % 2, (q // 2) % 2, q // 4
    order = (z, 1 + z % 2, 2 - 2 * (z % 2) + z // 2, 3 - 3 * (z // 2))

    def device(nz, fa, fb, core):
        fx, fy = fa * (1 - c) + fb * c, fb * (1 - c) + fa * c
        nx, ny = x + fx * (1 - 2 * x), y + fy * (1 - 2 * y)
        return (nz * 4 + ny * 2 + nx, core)

    column = [device(order[i], 0, 0, c) for i in range(1, 4)]
    a_side, b_side, partner = device(z, 1, 0, c), device(z, 0, 1, c), device(z, 0, 0, 1 - c)
    diagonal = device(z, 1, 1, c)
    near = column + [a_side, b_side, diagonal, partner]

    barrier = pltpu.get_barrier_semaphore()

    for d in near:
        pl.semaphore_signal(barrier, inc=1, device_id=d, device_id_type=MESH)

    loads = [pltpu.make_async_copy(src, dst, load_sem.at[i]) for i, (src, dst) in enumerate(
        ((hidden_hbm, hidden), (gain_hbm, gain), (target_hbm, target_row), (mask_hbm, mask),
         (length_hbm, length), (emb_hbm, emb)))]
    for copy in loads:
        copy.start()
    for copy in loads[:3]:
        copy.wait()
    rows = hidden[...].astype(jnp.float32)
    scale = lax.rsqrt(jnp.mean(rows * rows, axis=1, keepdims=True) + 1e-06)
    own = pl.ds(pl.multiple_of(z * 8 * slots, slots), slots)
    X[own, 0:width] = (rows * scale * gain[...]).astype(jnp.bfloat16)
    tgt = jnp.broadcast_to(target_row[...], (slots, slots))
    eye = lax.broadcasted_iota(jnp.int32, (slots, slots), 0) == lax.broadcasted_iota(
        jnp.int32, (slots, slots), 1)
    tcol = jnp.sum(jnp.where(eye, tgt, 0).astype(jnp.float32), axis=1, keepdims=True)
    high = jnp.floor(tcol * (1.0 / 256.0))
    low = tcol - high * 256.0
    lane = lax.broadcasted_iota(jnp.int32, (slots, 128), 1)
    X[own, width:width + 128] = jnp.where(
        lane == 0, high, jnp.where(lane == 1, low, 0.0)).astype(jnp.bfloat16)
    pl.semaphore_wait(barrier, len(near))

    piece = slots // PARTS

    def block(slot, h):
        return X.at[pl.ds(pl.multiple_of(slot * slots + h * piece, piece), piece), :]

    def copy_of(src, dst, h, send_sem, dev):
        return pltpu.make_async_remote_copy(
            src_ref=block(src, h), dst_ref=block(dst, h), send_sem=send_sem,
            recv_sem=xr.at[dst, h], device_id=dev, device_id_type=MESH)

    def copies(b, a, i, h):
        s, here, out = order[i], J(b, a, 0, order[i]), []
        if b + a + i == 0:
            for n in (0, 1, 2):
                out.append(copy_of(here, here, h, z_sem.at[n, h], column[n]))
        if b + a == 0:
            out.append(copy_of(here, J(0, 1, 0, s), h, a_sem.at[i, h], a_side))
            out.append(copy_of(here, J(1, 0, 0, s), h, b_sem.at[i, h], b_side))
            if i not in RELAYED:
                out.append(copy_of(here, J(1, 1, 0, s), h, c_sem.at[i, h], diagonal))
        if b == 0 and a == 1 and i in RELAYED:
            out.append(copy_of(here, J(1, 1, 0, s), h, c_sem.at[i, h], b_side))
        out.append(copy_of(here, J(b, a, 1, s), h, p_sem.at[i * 4 + b * 2 + a, h], partner))
        return out

    sends = []

    def forward(b, a, i, h):
        for copy in copies(b, a, i, h):
            copy.start()
            sends.append(copy)

    def arrived(slot, h):
        copy_of(slot, slot, h, p_sem.at[0, h], partner).wait_recv()

    def relay(b, a, i):
        for h in range(PARTS):
            arrived(J(b, a, 0, order[i]), h)
            forward(b, a, i, h)

    start = ((q * 2 + c) * voc).astype(jnp.float32)
    outs = []

    def group(i):
        for b in range(2):
            for a in range(2):
                for h in range(PARTS):
                    arrived(J(b, a, 1, order[i]), h)
        toks = 8 * slots
        base = pl.multiple_of(order[i] * toks, toks)
        pick = lax.broadcasted_iota(jnp.int32, (8, 128), 1)
        pick = jnp.where(pick == 0, 256.0, jnp.where(pick == 1, 1.0, 0.0)).astype(jnp.bfloat16)
        target = lax.dot_general(
            pick, X[pl.ds(base, toks), width:width + 128], (((1,), (1,)), ((), ())),
            preferred_element_type=jnp.float32)[0:1, :] - start
        raw = lax.dot_general(
            emb[...], X[pl.ds(base, toks), 0:width], (((1,), (1,)), ((), ())),
            preferred_element_type=jnp.float32)
        logits = 30.0 * jnp.tanh(raw / 30.0)
        expo = jnp.exp(logits)
        ident = lax.broadcasted_iota(jnp.int32, (voc, toks), 0).astype(jnp.float32)
        part[i, 0:1, :] = jnp.sum(expo, axis=0, keepdims=True)
        part[i, 1:2, :] = jnp.sum(expo * logits, axis=0, keepdims=True)
        part[i, 2:3, :] = jnp.sum(jnp.where(ident == target, logits, 0.0), axis=0, keepdims=True)
        part[i, 3:4, :] = jnp.zeros((1, toks), jnp.float32)
        for k in range(7, -1, -1):
            if i + k == 0:
                continue
            b, a, area = k // 4, k // 2 % 2, k % 2
            fa, fb = (a, b) if area == 0 else (b, a)
            copy = pltpu.make_async_remote_copy(
                src_ref=part.at[i], dst_ref=R.at[z * 8 + k], send_sem=rs.at[i * 8 + k],
                recv_sem=rr.at[z * 8 + k],
                device_id=device(order[i], fa, fb, c if area == 0 else 1 - c),
                device_id_type=MESH)
            copy.start()
            outs.append((copy, order[i] * 8 + k))

    for h in range(PARTS):
        forward(0, 0, 0, h)
    relay(0, 0, 1)
    relay(0, 1, 0)
    relay(1, 0, 0)
    relay(0, 0, 2)
    relay(1, 1, 0)
    relay(0, 0, 3)
    for copy in loads[3:]:
        copy.wait()
    group(0)
    for b, a in ((0, 1), (1, 0), (1, 1)):
        relay(b, a, 1)
    group(1)
    for b, a in ((0, 1), (1, 0), (1, 1)):
        relay(b, a, 2)
    group(2)
    for b, a in ((0, 1), (1, 0), (1, 1)):
        relay(b, a, 3)
    group(3)

    for _, slot in outs:
        pltpu.make_async_remote_copy(
            src_ref=part.at[0], dst_ref=R.at[slot], send_sem=rs.at[0], recv_sem=rr.at[slot],
            device_id=partner, device_id_type=MESH).wait_recv()
    R[z * 8] = part[0]
    home = lax.broadcasted_iota(jnp.int32, (4, 8 * slots), 1) // slots
    acc = jnp.zeros((4, 8 * slots), jnp.float32)
    for k in range(8):
        acc = acc + jnp.where(home == k, (R[k] + R[8 + k]) + (R[16 + k] + R[24 + k]), 0.0)
    for shift in (64, 32, 16):
        acc = acc + pltpu.roll(acc, shift, 1)
    total, moment, picked = (acc[i:i + 1, 0:slots] for i in range(3))
    lse = jnp.log(total)
    position = c * slots + lax.broadcasted_iota(jnp.int32, (1, slots), 1)
    scored = (mask[...] == 1) & (position < length[0])
    out_ref[0:1, :] = jnp.where(scored, picked - lse, 0.0)
    out_ref[1:2, :] = jnp.where(scored, lse - moment / total, 0.0)

    for copy in sends:
        copy.wait_send()
    for copy, _ in outs:
        copy.wait_send()


def fused(hidden, norm_gain, embedding, target_ids, lengths, response_mask):
    _, slots, width = hidden.shape
    voc = embedding.shape[0]
    anywhere = pl.BlockSpec(memory_space=pl.ANY)
    dma = pltpu.SemaphoreType.DMA
    out = pl.pallas_call(
        functools.partial(kernel, slots),
        out_shape=jax.ShapeDtypeStruct((2, slots), jnp.float32),
        in_specs=[anywhere] * 6,
        out_specs=pl.BlockSpec(memory_space=pltpu.VMEM),
        scratch_shapes=[
            pltpu.VMEM((slots, width), jnp.bfloat16),
            pltpu.VMEM((1, width), jnp.float32),
            pltpu.VMEM((1, slots), jnp.int32),
            pltpu.VMEM((1, slots), jnp.int32),
            pltpu.SMEM((1,), jnp.int32),
            pltpu.VMEM((voc, width), jnp.bfloat16),
            pltpu.VMEM((32 * slots, width + 128), jnp.bfloat16),
            pltpu.VMEM((4, 4, 8 * slots), jnp.float32),
            pltpu.VMEM((32, 4, 8 * slots), jnp.float32),
            dma((6,)), dma((3, PARTS)), dma((4, PARTS)), dma((4, PARTS)), dma((4, PARTS)),
            dma((16, PARTS)), dma((32, PARTS)), dma((32,)), dma((32,)),
        ],
        compiler_params=pltpu.CompilerParams(collective_id=0, has_side_effects=True),
    )(hidden.reshape(slots, width), norm_gain.reshape(1, width), target_ids, response_mask,
      lengths, embedding)
    return (out[0:1], out[1:2])


def solution(mesh):
    body = fused if dict(mesh.shape) == {"req": 16, "tp": 2} else on_device
    return jax.shard_map(body, mesh=mesh, **SPECS)
```

```python
import functools

import jax
import jax.numpy as jnp
from jax import lax
from jax.experimental import pallas as pl
from jax.experimental.pallas import tpu as pltpu
from jax.sharding import PartitionSpec as P

MESH = pl.DeviceIdType.MESH
SPECS = dict(
    in_specs=(
        P("req", "tp", None),
        P(),
        P(("req", "tp"), None),
        P("req", "tp"),
        P("req"),
        P("req", "tp"),
    ),
    out_specs=(P("req", "tp"), P("req", "tp")),
    check_vma=False,
)


def vocab_sums(states, targets, table, vocab_start):
    raw = lax.dot_general(
        states, table, (((1,), (1,)), ((), ())), preferred_element_type=jnp.float32
    )
    logits = 30.0 * jnp.tanh(raw / 30.0)
    expo = jnp.exp(logits)
    ident = vocab_start + lax.broadcasted_iota(jnp.int32, (1, table.shape[0]), 1)
    hit = jnp.where(ident == targets[:, None], logits, jnp.float32(0.0))
    return (jnp.sum(expo, axis=1), jnp.sum(expo * logits, axis=1), jnp.sum(hit, axis=1))


def on_device(hidden, norm_gain, embedding, target_ids, lengths, response_mask):
    seq_here, slots, width = hidden.shape
    rows = hidden.reshape(seq_here * slots, width).astype(jnp.float32)
    scale = lax.rsqrt(jnp.mean(rows * rows, axis=1, keepdims=True) + 1e-06)
    normed = (rows * scale * norm_gain[None, :]).astype(jnp.bfloat16)
    targets = target_ids.reshape(seq_here * slots)
    vocab_start = lax.axis_index(("req", "tp")) * embedding.shape[0]
    sums = vocab_sums(
        lax.all_gather(normed, ("req", "tp"), axis=0, tiled=True),
        lax.all_gather(targets, ("req", "tp"), axis=0, tiled=True),
        embedding,
        vocab_start,
    )
    total, moment, picked = (
        lax.psum_scatter(s, ("req", "tp"), scatter_dimension=0, tiled=True) for s in sums
    )
    lse = jnp.log(total)
    position = lax.axis_index("tp") * slots + lax.broadcasted_iota(jnp.int32, (seq_here, slots), 1)
    scored = (response_mask == 1) & (position < lengths[:, None])
    logprob = jnp.where(scored, (picked - lse).reshape(seq_here, slots), jnp.float32(0.0))
    entropy = jnp.where(scored, (lse - moment / total).reshape(seq_here, slots), jnp.float32(0.0))
    return (logprob, entropy)


PARTS = 1
RELAYED = ()


def J(b, a, area, s):
    return s * 8 + b * 4 + a * 2 + area


def kernel(slots, hidden_hbm, gain_hbm, target_hbm, mask_hbm, length_hbm, emb_hbm, out_ref,
           hidden, gain, target_row, mask, length, emb, X, part, R,
           load_sem, z_sem, a_sem, b_sem, c_sem, p_sem, xr, rs, rr):
    width = hidden.shape[1]
    voc = emb.shape[0]
    q, c = lax.axis_index("req"), lax.axis_index("tp")
    x, y, z = q % 2, (q // 2) % 2, q // 4
    order = (z, 1 + z % 2, 2 - 2 * (z % 2) + z // 2, 3 - 3 * (z // 2))

    def device(nz, fa, fb, core):
        fx, fy = fa * (1 - c) + fb * c, fb * (1 - c) + fa * c
        nx, ny = x + fx * (1 - 2 * x), y + fy * (1 - 2 * y)
        return (nz * 4 + ny * 2 + nx, core)

    column = [device(order[i], 0, 0, c) for i in range(1, 4)]
    a_side, b_side, partner = device(z, 1, 0, c), device(z, 0, 1, c), device(z, 0, 0, 1 - c)
    diagonal = device(z, 1, 1, c)
    near = column + [a_side, b_side, diagonal, partner]

    barrier = pltpu.get_barrier_semaphore()

    for d in near:
        pl.semaphore_signal(barrier, inc=1, device_id=d, device_id_type=MESH)

    loads = [pltpu.make_async_copy(src, dst, load_sem.at[i]) for i, (src, dst) in enumerate(
        ((hidden_hbm, hidden), (gain_hbm, gain), (target_hbm, target_row), (mask_hbm, mask),
         (length_hbm, length), (emb_hbm, emb)))]
    for copy in loads:
        copy.start()
    for copy in loads[:3]:
        copy.wait()
    rows = hidden[...].astype(jnp.float32)
    scale = lax.rsqrt(jnp.mean(rows * rows, axis=1, keepdims=True) + 1e-06)
    own = pl.ds(pl.multiple_of(z * 8 * slots, slots), slots)
    X[own, 0:width] = (rows * scale * gain[...]).astype(jnp.bfloat16)
    tgt = jnp.broadcast_to(target_row[...], (slots, slots))
    eye = lax.broadcasted_iota(jnp.int32, (slots, slots), 0) == lax.broadcasted_iota(
        jnp.int32, (slots, slots), 1)
    tcol = jnp.sum(jnp.where(eye, tgt, 0).astype(jnp.float32), axis=1, keepdims=True)
    high = jnp.floor(tcol * (1.0 / 256.0))
    low = tcol - high * 256.0
    lane = lax.broadcasted_iota(jnp.int32, (slots, 128), 1)
    X[own, width:width + 128] = jnp.where(
        lane == 0, high, jnp.where(lane == 1, low, 0.0)).astype(jnp.bfloat16)
    pl.semaphore_wait(barrier, len(near))

    piece = slots // PARTS

    def block(slot, h):
        return X.at[pl.ds(pl.multiple_of(slot * slots + h * piece, piece), piece), :]

    def copy_of(src, dst, h, send_sem, dev):
        return pltpu.make_async_remote_copy(
            src_ref=block(src, h), dst_ref=block(dst, h), send_sem=send_sem,
            recv_sem=xr.at[dst, h], device_id=dev, device_id_type=MESH)

    def copies(b, a, i, h):
        s, here, out = order[i], J(b, a, 0, order[i]), []
        if b + a + i == 0:
            for n in (0, 1, 2):
                out.append(copy_of(here, here, h, z_sem.at[n, h], column[n]))
        if b + a == 0:
            if i not in RELAYED:
                out.append(copy_of(here, J(1, 1, 0, s), h, c_sem.at[i, h], diagonal))
            out.append(copy_of(here, J(0, 1, 0, s), h, a_sem.at[i, h], a_side))
            out.append(copy_of(here, J(1, 0, 0, s), h, b_sem.at[i, h], b_side))
        if b == 0 and a == 1 and i in RELAYED:
            out.append(copy_of(here, J(1, 1, 0, s), h, c_sem.at[i, h], b_side))
        out.append(copy_of(here, J(b, a, 1, s), h, p_sem.at[i * 4 + b * 2 + a, h], partner))
        return out

    sends = []

    def forward(b, a, i, h):
        for copy in copies(b, a, i, h):
            copy.start()
            sends.append(copy)

    def arrived(slot, h):
        copy_of(slot, slot, h, p_sem.at[0, h], partner).wait_recv()

    def relay(b, a, i):
        for h in range(PARTS):
            arrived(J(b, a, 0, order[i]), h)
            forward(b, a, i, h)

    start = ((q * 2 + c) * voc).astype(jnp.float32)
    outs = []

    def group(i):
        for b in range(2):
            for a in range(2):
                for h in range(PARTS):
                    arrived(J(b, a, 1, order[i]), h)
        toks = 8 * slots
        base = pl.multiple_of(order[i] * toks, toks)
        pick = lax.broadcasted_iota(jnp.int32, (8, 128), 1)
        pick = jnp.where(pick == 0, 256.0, jnp.where(pick == 1, 1.0, 0.0)).astype(jnp.bfloat16)
        target = lax.dot_general(
            pick, X[pl.ds(base, toks), width:width + 128], (((1,), (1,)), ((), ())),
            preferred_element_type=jnp.float32)[0:1, :] - start
        raw = lax.dot_general(
            emb[...], X[pl.ds(base, toks), 0:width], (((1,), (1,)), ((), ())),
            preferred_element_type=jnp.float32)
        logits = 30.0 * jnp.tanh(raw / 30.0)
        expo = jnp.exp(logits)
        ident = lax.broadcasted_iota(jnp.int32, (voc, toks), 0).astype(jnp.float32)
        part[i, 0:1, :] = jnp.sum(expo, axis=0, keepdims=True)
        part[i, 1:2, :] = jnp.sum(expo * logits, axis=0, keepdims=True)
        part[i, 2:3, :] = jnp.sum(jnp.where(ident == target, logits, 0.0), axis=0, keepdims=True)
        part[i, 3:4, :] = jnp.zeros((1, toks), jnp.float32)
        for k in range(7, -1, -1):
            if i + k == 0:
                continue
            b, a, area = k // 4, k // 2 % 2, k % 2
            fa, fb = (a, b) if area == 0 else (b, a)
            copy = pltpu.make_async_remote_copy(
                src_ref=part.at[i], dst_ref=R.at[z * 8 + k], send_sem=rs.at[i * 8 + k],
                recv_sem=rr.at[z * 8 + k],
                device_id=device(order[i], fa, fb, c if area == 0 else 1 - c),
                device_id_type=MESH)
            copy.start()
            outs.append((copy, order[i] * 8 + k))

    for h in range(PARTS):
        forward(0, 0, 0, h)
    relay(0, 0, 1)
    relay(0, 1, 0)
    relay(1, 0, 0)
    relay(0, 0, 2)
    relay(1, 1, 0)
    relay(0, 0, 3)
    for copy in loads[3:]:
        copy.wait()
    group(0)
    relay(0, 1, 1)
    relay(1, 0, 1)
    relay(1, 1, 1)
    relay(0, 1, 2)
    relay(1, 0, 2)
    relay(1, 1, 2)
    group(1)
    relay(0, 1, 3)
    relay(1, 0, 3)
    relay(1, 1, 3)
    group(2)
    group(3)
    for _, slot in outs:
        pltpu.make_async_remote_copy(
            src_ref=part.at[0], dst_ref=R.at[slot], send_sem=rs.at[0], recv_sem=rr.at[slot],
            device_id=partner, device_id_type=MESH).wait_recv()
    R[z * 8] = part[0]
    home = lax.broadcasted_iota(jnp.int32, (4, 8 * slots), 1) // slots
    acc = jnp.zeros((4, 8 * slots), jnp.float32)
    for k in range(8):
        acc = acc + jnp.where(home == k, (R[k] + R[8 + k]) + (R[16 + k] + R[24 + k]), 0.0)
    for shift in (64, 32, 16):
        acc = acc + pltpu.roll(acc, shift, 1)
    total, moment, picked = (acc[i:i + 1, 0:slots] for i in range(3))
    lse = jnp.log(total)
    position = c * slots + lax.broadcasted_iota(jnp.int32, (1, slots), 1)
    scored = (mask[...] == 1) & (position < length[0])
    out_ref[0:1, :] = jnp.where(scored, picked - lse, 0.0)
    out_ref[1:2, :] = jnp.where(scored, lse - moment / total, 0.0)

    for copy in sends:
        copy.wait_send()
    for copy, _ in outs:
        copy.wait_send()


def fused(hidden, norm_gain, embedding, target_ids, lengths, response_mask):
    _, slots, width = hidden.shape
    voc = embedding.shape[0]
    anywhere = pl.BlockSpec(memory_space=pl.ANY)
    dma = pltpu.SemaphoreType.DMA
    out = pl.pallas_call(
        functools.partial(kernel, slots),
        out_shape=jax.ShapeDtypeStruct((2, slots), jnp.float32),
        in_specs=[anywhere] * 6,
        out_specs=pl.BlockSpec(memory_space=pltpu.VMEM),
        scratch_shapes=[
            pltpu.VMEM((slots, width), jnp.bfloat16),
            pltpu.VMEM((1, width), jnp.float32),
            pltpu.VMEM((1, slots), jnp.int32),
            pltpu.VMEM((1, slots), jnp.int32),
            pltpu.SMEM((1,), jnp.int32),
            pltpu.VMEM((voc, width), jnp.bfloat16),
            pltpu.VMEM((32 * slots, width + 128), jnp.bfloat16),
            pltpu.VMEM((4, 4, 8 * slots), jnp.float32),
            pltpu.VMEM((32, 4, 8 * slots), jnp.float32),
            dma((6,)), dma((3, PARTS)), dma((4, PARTS)), dma((4, PARTS)), dma((4, PARTS)),
            dma((16, PARTS)), dma((32, PARTS)), dma((32,)), dma((32,)),
        ],
        compiler_params=pltpu.CompilerParams(collective_id=0, has_side_effects=True),
    )(hidden.reshape(slots, width), norm_gain.reshape(1, width), target_ids, response_mask,
      lengths, embedding)
    return (out[0:1], out[1:2])


def solution(mesh):
    body = fused if dict(mesh.shape) == {"req": 16, "tp": 2} else on_device
    return jax.shard_map(body, mesh=mesh, **SPECS)
```
